32 devices in a mesh: group: 2 (over x), tm: 16 (over z, y, core).
Axes of the slice: x: 2, y: 2, z: 4, core: 2. Of those that a mesh axis runs over, the one named last changes fastest.
Arguments:
- noise: float32 [8, 4096], P('group'), parts along dimension 0, may hold values from -6 to 6
- labels: int32 [8], P('group'), parts along dimension 0, may hold values from 0 to 1000
- timesteps: int32 [25], replicated, may hold values from 0 to 399, as said below
- window_start: int32 [1], replicated, may hold values from 0 to 8
- time_weight_in: bfloat16 [256, 768], replicated, may hold values from -0.375 to 0.375
- time_weight_out: bfloat16 [768, 768], replicated, may hold values from -0.21875 to 0.21875
- class_table: bfloat16 [1001, 768], replicated, may hold values from -6 to 6
- patch_weight: bfloat16 [64, 768], replicated, may hold values from -0.75 to 0.75
- query_key_value: bfloat16 [1, 768, 2304], P(None, None, 'tm'), may hold values from -0.21875 to 0.21875
- mix_weight: bfloat16 [1, 768, 768], P(None, None, 'tm'), may hold values from -0.21875 to 0.21875
- expand_weight: bfloat16 [1, 768, 3072], P(None, None, 'tm'), may hold values from -0.21875 to 0.21875
- shrink_weight: bfloat16 [1, 3072, 768], P(None, None, 'tm'), may hold values from -0.109375 to 0.109375
- block_modulation: bfloat16 [1, 768, 4608], P(None, None, 'tm'), may hold values from -0.21875 to 0.21875
- final_modulation: bfloat16 [768, 1536], P(None, 'tm'), may hold values from -0.21875 to 0.21875
- output_weight: bfloat16 [768, 64], replicated, may hold values from -0.21875 to 0.21875
Outputs:
- trajectory: float32 [16, 8, 4096], P('tm', 'group'), parts along dimension 1
The draws below stay inside these ranges and needn't reach their ends.
There are 2 independent parts, one for each index of `group`. The reference program is written for one: setup_inputs(seed, part) draws one part's arguments, and reference() takes and returns one part's arrays. A program takes and returns all parts, laid end to end along the dimension named above; an argument that names none is the same for every part. Nothing has to cross between parts.
Inputs may be any that keep to these rules, and one draw needn't show every extreme that they name: `timesteps`: strictly decreasing; the first entry is 399 and the last is 0.
All inputs are finite; a program needn't handle non-finite values.
Results may differ from the reference program's by a relative error of at most 0.0025.
Values may be sent and summed in bfloat16 or wider, within the bound.
A program may use at most 128 MiB of HBM per device.

```python
import math
import jax
import jax.numpy as jnp
from jax import lax

D = 768
FF = 3072
HEADS = 12
PATCH_DIM = 64
CLASSES = 1000
FREQ = 256
SAMPLES = 4
LAYERS = 1
ITERS = 2
TRAIN_T = 1000
SPAN = 400
EXTRA = 8
LATENT = 4096
STEPS = 16
SCHED = 25


def draw_timesteps(key, part):
    inner = jax.random.permutation(key, SPAN - 2)[:SCHED - 2] + 1
    ordered = -jnp.sort(-inner)
    first = jnp.full((1,), SPAN - 1, dtype=jnp.int32)
    last = jnp.zeros((1,), dtype=jnp.int32)
    return jnp.concatenate([first, ordered.astype(jnp.int32), last])


def touch_ends(values, stream_key, smallest, high):
    longest = values.shape.index(max(values.shape))
    spots = []
    for shift in (0, 1):
        where = [jax.random.randint(jax.random.fold_in(stream_key, axis), (), 0, length) for axis, length in enumerate(values.shape)]
        where[longest] = (where[longest] + shift) % values.shape[longest]
        spots.append(tuple(where))
    return values.at[spots[0]].set(smallest).at[spots[1]].set(high)


def steps_of(own_key, dims, split, smallest, high):
    gain, own = 1.0, jax.random.fold_in(own_key, 6)
    for dim, blocks in split:
        heights = jnp.exp(jax.random.uniform(jax.random.fold_in(own, dim), (blocks,), jnp.float32, smallest / len(split), high / len(split)))
        gain = gain * jnp.repeat(heights, dims[dim] // blocks).reshape([-1 if axis == dim else 1 for axis in range(len(dims))])
    return gain


def gaussian(own_key, shape, spread, bound, split=(), kind=jnp.bfloat16):
    values = jax.random.normal(own_key, shape, jnp.float32) * spread
    if len(split) > 0:
        values = steps_of(own_key, shape, split, -0.22, 0.18) * values
    return jnp.clip(values, min=-bound, max=bound).astype(kind)


def setup_inputs(seed: int = 0, part: int = 0) -> dict:
    arg_keys = jax.random.split(jax.random.key(seed), 16)
    part_keys = jax.random.split(jax.random.fold_in(arg_keys[15], part), 16)
    noise = gaussian(part_keys[0], (SAMPLES, LATENT), 1.0, 6.0, (), jnp.float32)
    labels = touch_ends(jax.random.randint(part_keys[1], (SAMPLES,), 0, CLASSES + 1), jax.random.fold_in(part_keys[1], 1), 0, CLASSES).astype(jnp.int32)
    timesteps = draw_timesteps(jax.random.fold_in(arg_keys[15], 71), part)
    window_start = jax.random.randint(arg_keys[3], (1,), 0, EXTRA + 1).astype(jnp.int32)
    time_weight_in = gaussian(arg_keys[4], (FREQ, D), FREQ ** -0.5, 0.375)
    time_weight_out = gaussian(arg_keys[5], (D, D), D ** -0.5, 0.21875)
    class_table = gaussian(arg_keys[6], (CLASSES + 1, D), 1.0, 6.0)
    patch_weight = gaussian(arg_keys[7], (PATCH_DIM, D), PATCH_DIM ** -0.5, 0.75)
    query_key_value = gaussian(arg_keys[8], (LAYERS, D, 3 * D), D ** -0.5, 0.21875, ((2, 16),))
    mix_weight = gaussian(arg_keys[9], (LAYERS, D, D), D ** -0.5, 0.21875, ((2, 16),))
    expand_weight = gaussian(arg_keys[10], (LAYERS, D, FF), D ** -0.5, 0.21875, ((2, 16),))
    shrink_weight = gaussian(arg_keys[11], (LAYERS, FF, D), FF ** -0.5, 0.109375, ((2, 16),))
    block_modulation = gaussian(arg_keys[12], (LAYERS, D, 6 * D), D ** -0.5, 0.21875, ((2, 16),))
    final_modulation = gaussian(arg_keys[13], (D, 2 * D), D ** -0.5, 0.21875, ((1, 16),))
    output_weight = gaussian(arg_keys[14], (D, PATCH_DIM), D ** -0.5, 0.21875)
    return dict(noise=noise, labels=labels, timesteps=timesteps, window_start=window_start, time_weight_in=time_weight_in, time_weight_out=time_weight_out, class_table=class_table, patch_weight=patch_weight, query_key_value=query_key_value, mix_weight=mix_weight, expand_weight=expand_weight, shrink_weight=shrink_weight, block_modulation=block_modulation, final_modulation=final_modulation, output_weight=output_weight)


def layer_norm(values):
    average = lax.optimization_barrier(jnp.mean(values, axis=-1, keepdims=True))
    centered = values - average
    variance = lax.optimization_barrier(jnp.mean(centered * centered, axis=-1, keepdims=True))
    return centered / jnp.sqrt(variance + 1e-06)

def position_table(count, width):
    side = math.isqrt(count)
    quarter = width // 4
    omega = 1.0 / 10000.0 ** (jnp.arange(quarter, dtype=jnp.float32) / quarter)
    index = jnp.arange(count, dtype=jnp.int32)
    first = (index // side).astype(jnp.float32)[:, None] * omega[None, :]
    second = (index % side).astype(jnp.float32)[:, None] * omega[None, :]
    return jnp.concatenate([jnp.sin(first), jnp.cos(first), jnp.sin(second), jnp.cos(second)], axis=1)

def plan_terms(timesteps, window_start, step_index, train_steps):
    levels = jnp.arange(train_steps, dtype=jnp.float32)
    betas = 0.0001 + (0.02 - 0.0001) * levels / (train_steps - 1)
    alpha_bar = jnp.cumprod(1.0 - betas)
    current = jnp.take(timesteps, window_start[0] + step_index)
    following = jnp.take(timesteps, window_start[0] + step_index + 1)
    bar_current = jnp.take(alpha_bar, current)
    bar_following = jnp.take(alpha_bar, following)
    scale_state = jnp.sqrt(bar_following / bar_current)
    scale_noise = jnp.sqrt(1.0 - bar_following) - scale_state * jnp.sqrt(1.0 - bar_current)
    return (current, scale_state, scale_noise)

def conditioning(current, labels, time_weight_in, time_weight_out, class_table):
    half = time_weight_in.shape[0] // 2
    rates = jnp.exp(-math.log(10000.0) * jnp.arange(half, dtype=jnp.float32) / half)
    angles = current.astype(jnp.float32)[:, None] * rates[None, :]
    features = jnp.concatenate([jnp.cos(angles), jnp.sin(angles)], axis=1).astype(jnp.bfloat16)
    time_hidden = jax.nn.silu(jnp.dot(features, time_weight_in, preferred_element_type=jnp.float32)).astype(jnp.bfloat16)
    time_embed = jnp.dot(time_hidden, time_weight_out, preferred_element_type=jnp.float32)
    selector = (labels[:, None] == jnp.arange(class_table.shape[0], dtype=jnp.int32)[None, :]).astype(jnp.bfloat16)
    class_embed = jnp.dot(selector, class_table, preferred_element_type=jnp.float32)
    return jax.nn.silu(time_embed[:, None, :] + class_embed[None, :, :]).astype(jnp.bfloat16)

def network(states, block_terms, final_terms, patch_weight, query_key_value, mix_weight, expand_weight, shrink_weight, output_weight, heads):
    count = states.shape[0]
    patch = patch_weight.shape[0]
    width = patch_weight.shape[1]
    tokens = states.shape[1] // patch
    head_dim = width // heads
    patches = states.reshape(count * tokens, patch).astype(jnp.bfloat16)
    hidden = jnp.dot(patches, patch_weight, preferred_element_type=jnp.float32).reshape(count, tokens, width)
    hidden = hidden + position_table(tokens, width)[None]
    for layer in range(block_terms.shape[0]):
        blocks = block_terms[layer].reshape(count, 6, 1, width)
        normed = (layer_norm(hidden) * (1.0 + blocks[:, 1]) + blocks[:, 0]).astype(jnp.bfloat16)
        projected = jnp.dot(normed.reshape(count * tokens, width), query_key_value[layer], preferred_element_type=jnp.float32).astype(jnp.bfloat16)
        projected = projected.reshape(count, tokens, 3, heads, head_dim).astype(jnp.float32)
        scores = jnp.einsum('rqhd,rkhd->rhqk', projected[:, :, 0], projected[:, :, 1]) / math.sqrt(head_dim)
        raised = jnp.exp(scores)
        weights = (raised / lax.optimization_barrier(jnp.sum(raised, axis=-1, keepdims=True))).astype(jnp.bfloat16)
        attended = jnp.einsum('rhqk,rkhd->rqhd', weights.astype(jnp.float32), projected[:, :, 2]).astype(jnp.bfloat16)
        mixed = jnp.dot(attended.reshape(count * tokens, width), mix_weight[layer], preferred_element_type=jnp.float32)
        hidden = hidden + blocks[:, 2] * mixed.reshape(count, tokens, width)
        normed = (layer_norm(hidden) * (1.0 + blocks[:, 4]) + blocks[:, 3]).astype(jnp.bfloat16)
        expanded = jax.nn.gelu(jnp.dot(normed.reshape(count * tokens, width), expand_weight[layer], preferred_element_type=jnp.float32), approximate=True).astype(jnp.bfloat16)
        shrunk = jnp.dot(expanded, shrink_weight[layer], preferred_element_type=jnp.float32)
        hidden = hidden + blocks[:, 5] * shrunk.reshape(count, tokens, width)
    final = final_terms.reshape(count, 2, 1, width)
    normed = (layer_norm(hidden) * (1.0 + final[:, 1]) + final[:, 0]).astype(jnp.bfloat16)
    return jnp.dot(normed.reshape(count * tokens, width), output_weight, preferred_element_type=jnp.float32).reshape(count, tokens * patch)

def reference(noise, labels, timesteps, window_start, time_weight_in, time_weight_out, class_table, patch_weight, query_key_value, mix_weight, expand_weight, shrink_weight, block_modulation, final_modulation, output_weight):
    step_index = jnp.arange(STEPS, dtype=jnp.int32)
    current, scale_state, scale_noise = plan_terms(timesteps, window_start, step_index, TRAIN_T)
    condition = conditioning(current, labels, time_weight_in, time_weight_out, class_table)

    def one_step(item):
        rows, acting = item
        block_terms = jnp.einsum('rd,ldc->lrc', acting.astype(jnp.float32), block_modulation.astype(jnp.float32))
        final_terms = jnp.dot(acting, final_modulation, preferred_element_type=jnp.float32)
        return network(rows, block_terms, final_terms, patch_weight, query_key_value, mix_weight, expand_weight, shrink_weight, output_weight, HEADS)
    states = jnp.broadcast_to(noise[None], (STEPS,) + noise.shape)
    running = states
    for sweep in range(ITERS):
        predicted = lax.map(one_step, (states, condition))
        drift = (scale_state - 1.0)[:, None, None] * states + scale_noise[:, None, None] * predicted
        running = jnp.cumsum(drift, axis=0)
        states = noise[None] + running - drift
    return noise[None] + running
```

```python
import functools
import math

import jax
import jax.numpy as jnp
import numpy as np
from jax import lax
from jax.experimental import pallas as pl
from jax.experimental.pallas import tpu as pltpu
from jax.sharding import PartitionSpec as P

HEADS = 12
ITERS = 2
TRAIN_T = 1000


def carried_in(x, axis, combine, identity):
    count, index = (lax.axis_size(axis), lax.axis_index(axis))
    everything = lax.all_gather(x.astype(jnp.bfloat16), axis)
    start = jnp.broadcast_to(jnp.asarray(identity, x.dtype), x.shape)

    def hop(k, before):
        reached = k < index
        new = combine(before, everything[k].astype(x.dtype))
        return jnp.where(reached, new, before)

    return lax.fori_loop(0, count, hop, start)


def layer_norm(values):
    average = jnp.mean(values, axis=-1, keepdims=True)
    centered = values - average
    variance = jnp.mean(centered * centered, axis=-1, keepdims=True)
    return centered / jnp.sqrt(variance + 1e-06)


def position_table(count, width):
    side = math.isqrt(count)
    quarter = width // 4
    omega = 1.0 / 10000.0 ** (jnp.arange(quarter, dtype=jnp.float32) / quarter)
    index = jnp.arange(count, dtype=jnp.int32)
    first = (index // side).astype(jnp.float32)[:, None] * omega[None, :]
    second = (index % side).astype(jnp.float32)[:, None] * omega[None, :]
    return jnp.concatenate(
        [jnp.sin(first), jnp.cos(first), jnp.sin(second), jnp.cos(second)], axis=1
    )


def plan_terms(timesteps, window_start, step_index, train_steps):
    levels = jnp.arange(train_steps, dtype=jnp.float32)
    betas = 0.0001 + (0.02 - 0.0001) * levels / (train_steps - 1)
    alpha_bar = jnp.cumprod(1.0 - betas)
    current = jnp.take(timesteps, window_start[0] + step_index)
    following = jnp.take(timesteps, window_start[0] + step_index + 1)
    bar_current = jnp.take(alpha_bar, current)
    bar_following = jnp.take(alpha_bar, following)
    scale_state = jnp.sqrt(bar_following / bar_current)
    scale_noise = jnp.sqrt(1.0 - bar_following) - scale_state * jnp.sqrt(1.0 - bar_current)
    return (current, scale_state, scale_noise)


def conditioning(current, labels, time_weight_in, time_weight_out, class_table):
    half = time_weight_in.shape[0] // 2
    rates = jnp.exp(-math.log(10000.0) * jnp.arange(half, dtype=jnp.float32) / half)
    angles = current.astype(jnp.float32)[:, None] * rates[None, :]
    features = jnp.concatenate([jnp.cos(angles), jnp.sin(angles)], axis=1).astype(jnp.bfloat16)
    time_hidden = jax.nn.silu(
        jnp.dot(features, time_weight_in, preferred_element_type=jnp.float32)
    ).astype(jnp.bfloat16)
    time_embed = jnp.dot(time_hidden, time_weight_out, preferred_element_type=jnp.float32)
    selector = (
        labels[:, None] == jnp.arange(class_table.shape[0], dtype=jnp.int32)[None, :]
    ).astype(jnp.bfloat16)
    class_embed = jnp.dot(selector, class_table, preferred_element_type=jnp.float32)
    return jax.nn.silu(time_embed[:, None, :] + class_embed[None, :, :]).astype(jnp.bfloat16)


def network(
    states,
    block_terms,
    final_terms,
    patch_weight,
    query_key_value,
    mix_weight,
    expand_weight,
    shrink_weight,
    output_weight,
    heads,
):
    count = states.shape[0]
    patch = patch_weight.shape[0]
    width = patch_weight.shape[1]
    tokens = states.shape[1] // patch
    head_dim = width // heads
    patches = states.reshape(count * tokens, patch).astype(jnp.bfloat16)
    hidden = jnp.dot(patches, patch_weight, preferred_element_type=jnp.float32).reshape(
        count, tokens, width
    )
    hidden = hidden + position_table(tokens, width)[None]
    blocks = block_terms[0].reshape(count, 6, 1, width)
    normed = (layer_norm(hidden) * (1.0 + blocks[:, 1]) + blocks[:, 0]).astype(jnp.bfloat16)
    projected = jnp.dot(
        normed.reshape(count * tokens, width),
        query_key_value[0],
        preferred_element_type=jnp.float32,
    ).astype(jnp.bfloat16)
    projected = projected.reshape(count, tokens, 3, heads, head_dim)
    scores = jnp.einsum(
        "rqhd,rkhd->rhqk",
        projected[:, :, 0],
        projected[:, :, 1],
        preferred_element_type=jnp.float32,
    ) / math.sqrt(head_dim)
    raised = jnp.exp(scores)
    weights = (raised / jnp.sum(raised, axis=-1, keepdims=True)).astype(jnp.bfloat16)
    attended = jnp.einsum(
        "rhqk,rkhd->rqhd", weights, projected[:, :, 2], preferred_element_type=jnp.float32
    ).astype(jnp.bfloat16)
    mixed = jnp.dot(
        attended.reshape(count * tokens, width), mix_weight[0], preferred_element_type=jnp.float32
    )
    hidden = hidden + blocks[:, 2] * mixed.reshape(count, tokens, width)
    normed = (layer_norm(hidden) * (1.0 + blocks[:, 4]) + blocks[:, 3]).astype(jnp.bfloat16)
    expanded = jax.nn.gelu(
        jnp.dot(
            normed.reshape(count * tokens, width),
            expand_weight[0],
            preferred_element_type=jnp.float32,
        ),
        approximate=True,
    ).astype(jnp.bfloat16)
    shrunk = jnp.dot(expanded, shrink_weight[0], preferred_element_type=jnp.float32)
    hidden = hidden + blocks[:, 5] * shrunk.reshape(count, tokens, width)
    final = final_terms.reshape(count, 2, 1, width)
    normed = (layer_norm(hidden) * (1.0 + final[:, 1]) + final[:, 0]).astype(jnp.bfloat16)
    return jnp.dot(
        normed.reshape(count * tokens, width), output_weight, preferred_element_type=jnp.float32
    ).reshape(count, tokens * patch)


def add_terms(earlier, later):
    return earlier + later


def gathered_body(
    noise,
    labels,
    timesteps,
    window_start,
    time_weight_in,
    time_weight_out,
    class_table,
    patch_weight,
    query_key_value,
    mix_weight,
    expand_weight,
    shrink_weight,
    block_modulation,
    final_modulation,
    output_weight,
):
    position = lax.axis_index("tm")
    current, scale_state, scale_noise = plan_terms(timesteps, window_start, position[None], TRAIN_T)
    condition = conditioning(current, labels, time_weight_in, time_weight_out, class_table)[0]
    full_query, full_mix, full_expand, full_shrink = (
        lax.all_gather(query_key_value, "tm", axis=2, tiled=True),
        lax.all_gather(mix_weight, "tm", axis=2, tiled=True),
        lax.all_gather(expand_weight, "tm", axis=2, tiled=True),
        lax.all_gather(shrink_weight, "tm", axis=2, tiled=True),
    )
    everyone = lax.all_gather(condition, "tm", axis=0, tiled=True)
    block_part = jnp.einsum(
        "rd,ldc->lrc", everyone, block_modulation, preferred_element_type=jnp.float32
    )
    final_part = jnp.dot(everyone, final_modulation, preferred_element_type=jnp.float32)[None]
    block_terms, final_both = (
        lax.all_to_all(
            block_part.astype(jnp.bfloat16), "tm", split_axis=1, concat_axis=2, tiled=True
        ).astype(block_part.dtype),
        lax.all_to_all(
            final_part.astype(jnp.bfloat16), "tm", split_axis=1, concat_axis=2, tiled=True
        ).astype(final_part.dtype),
    )
    final_terms = final_both[0]
    states = noise
    running = noise
    for sweep in range(ITERS):
        predicted = network(
            states,
            block_terms,
            final_terms,
            patch_weight,
            full_query,
            full_mix,
            full_expand,
            full_shrink,
            output_weight,
            HEADS,
        )
        drift = (scale_state[0] - 1.0) * states + scale_noise[0] * predicted
        before = carried_in(drift, "tm", add_terms, jnp.zeros_like(drift))
        running = before + drift
        states = noise + before
    return (noise + running)[None]


PLANE = 4
PAD = 8
ROW_TILE = 256


def alpha_table():
    levels = np.arange(TRAIN_T, dtype=np.float64)
    return np.cumprod(1.0 - (0.0001 + (0.02 - 0.0001) * levels / (TRAIN_T - 1))).astype(np.float32)


def position_columns(count, width):
    side = math.isqrt(count)
    quarter = width // 4
    omega = 1.0 / 10000.0 ** (np.arange(quarter, dtype=np.float64) / quarter)
    index = np.arange(count)
    first = (index // side)[:, None] * omega[None, :]
    second = (index % side)[:, None] * omega[None, :]
    table = np.concatenate([np.sin(first), np.cos(first), np.sin(second), np.cos(second)], axis=1)
    return table.T.astype(np.float32)


def matmul(a, b):
    return jnp.dot(a, b, preferred_element_type=jnp.float32)


def kernel(
    n,
    samples,
    plan_ref,
    start_ref,
    alpha_ref,
    noise_ref,
    class_ref,
    tin_ref,
    tout_ref,
    modw_ref,
    patch_ref,
    outw_ref,
    pos_ref,
    q_ref,
    m_ref,
    e_ref,
    s_ref,
    out_ref,
    q_full,
    m_full,
    e_full,
    s_full,
    terms,
    hidden,
    projected,
    attended,
    expanded,
    mods_send,
    mods_recv,
    drift_send,
    drift_recv,
    total_send,
    total_recv,
    ring_recv,
    ring_send,
    x_recv,
    x_send,
    mate_recv,
    mate_send,
    local_sem,
    mods_sems,
    plane_sems,
    total_rsem,
    total_ssem,
):
    me, g = lax.axis_index("tm"), lax.axis_index("group")
    chips = n // 2
    half = chips // 2
    chip, core = lax.div(me, 2), lax.rem(me, 2)
    odd = lax.rem(chip, 2)
    pos = (1 - odd) * lax.div(chip, 2) + odd * (chips - 1 - lax.div(chip, 2))

    def device_at(place):
        place = lax.rem(place + chips, chips)
        upper = lax.div(place, half)
        where = (1 - upper) * (2 * place) + upper * (2 * (chips - 1 - place) + 1)
        return where * 2 + core

    right, left = {"tm": device_at(pos + 1)}, {"tm": device_at(pos - 1)}
    mate = {"tm": me + 1 - 2 * core}
    side = lax.rem(g, 2)
    xmate = {"group": g + 1 - 2 * side}
    fulls, shards = (q_full, m_full, e_full, s_full), (q_ref, m_ref, e_ref, s_ref)

    barrier = pltpu.get_barrier_semaphore()
    for off in range(1, n):
        pl.semaphore_signal(barrier, inc=1, device_id={"tm": lax.rem(me + off, n)}, device_id_type=pl.DeviceIdType.MESH)
    pl.semaphore_signal(barrier, inc=1, device_id=xmate, device_id_type=pl.DeviceIdType.MESH)
    pl.semaphore_wait(barrier, n)

    def send(src, dst, ssem, rsem, target):
        return pltpu.make_async_remote_copy(
            src_ref=src, dst_ref=dst, send_sem=ssem, recv_sem=rsem,
            device_id=target, device_id_type=pl.DeviceIdType.MESH,
        )

    def third(m):
        return shards[m].shape[0] // 3

    def part(m, owner, off, count):
        rows = shards[m].shape[0]
        return fulls[m].at[pl.ds(pl.multiple_of(owner * rows + off, 16), count)]

    def own(m, off, count):
        return shards[m].at[pl.ds(pl.multiple_of(off, 16), count)]

    def begin(m):
        t = third(m)
        off = side * t
        for way, target in ((0, right), (1, left)):
            send(own(m, off, 2 * t), part(m, me, off, 2 * t), ring_send.at[m], ring_recv.at[m, way, 0], target).start()
        send(shards[m], part(m, me, 0, 3 * t), mate_send.at[m], mate_recv.at[m], mate).start()
        pltpu.make_async_copy(shards[m], part(m, me, 0, 3 * t), local_sem.at[m]).start()

    def slab(m, way, hop):
        t = third(m)
        if hop < half:
            return side * t, 2 * t
        return side * t + way * t, t

    def take(m, hop):
        t = third(m)
        for way, target in ((0, right), (1, left)):
            owner = device_at(pos - hop) if way == 0 else device_at(pos + hop)
            off, count = slab(m, way, hop)
            here = part(m, owner, off, count)
            send(here, here, ring_send.at[m], ring_recv.at[m, way, hop - 1], target).wait_recv()
            if hop < half:
                onward = part(m, owner, *slab(m, way, hop + 1))
                send(onward, onward, ring_send.at[m], ring_recv.at[m, way, hop], target).start()
                across = part(m, owner, side * 2 * t, t)
                send(across, across, x_send.at[m], x_recv.at[m, 2 * (hop - 1) + way], xmate).start()
            send(here, here, mate_send.at[m], mate_recv.at[m], mate).start()
        if hop == half:
            across = part(m, device_at(pos + half), side * 2 * t, t)
            send(across, across, x_send.at[m], x_recv.at[m, 2 * (half - 1)], xmate).start()

    def take_across(m, hop):
        t = third(m)
        for way in ((0, 1) if hop < half else (0,)):
            owner = device_at(pos - hop) if way == 0 else device_at(pos + hop)
            here = part(m, owner, (1 - side) * 2 * t, t)
            send(here, here, x_send.at[m], x_recv.at[m, 2 * (hop - 1) + way], xmate).wait_recv()
            send(here, here, mate_send.at[m], mate_recv.at[m], mate).start()

    def settle(m):
        rows = shards[m].shape[0]
        everything = fulls[m].at[pl.ds(0, chips * rows)]
        send(everything, everything, mate_send.at[m], mate_recv.at[m], mate).wait_recv()
        pltpu.make_async_copy(shards[m], part(m, me, 0, rows), local_sem.at[m]).wait()

    def drain(m):
        t = third(m)
        for sem, count in ((ring_send, (4 * half - 2) * t), (x_send, (2 * half - 1) * t), (mate_send, 6 * half * t)):
            whole = fulls[m].at[pl.ds(0, count)]
            send(whole, whole, sem.at[m], mate_recv.at[m], mate).wait_send()

    begin(0)

    width = tin_ref.shape[1]
    freq = tin_ref.shape[0]
    first = start_ref[0]
    step_of = lax.broadcasted_iota(jnp.int32, (n * PAD, freq // 2), 0) // PAD
    current = jnp.zeros((n * PAD, freq // 2), jnp.float32)
    for j in range(n):
        current = jnp.where(step_of == j, plan_ref[first + j].astype(jnp.float32), current)
    lane = lax.broadcasted_iota(jnp.int32, (n * PAD, freq // 2), 1).astype(jnp.float32)
    angles = current * jnp.exp(-math.log(10000.0) * lane / (freq // 2))
    features = jnp.concatenate([jnp.cos(angles), jnp.sin(angles)], axis=1).astype(jnp.bfloat16)
    time_hidden = jax.nn.silu(matmul(features, tin_ref[...])).astype(jnp.bfloat16)
    classes = class_ref[...].astype(jnp.float32)
    summed = matmul(time_hidden, tout_ref[...]) + jnp.concatenate([classes] * n, axis=0)
    condition = jax.nn.silu(summed).astype(jnp.bfloat16)
    columns = modw_ref.shape[1]
    mods_send[...] = matmul(condition, modw_ref[...]).reshape(n, PAD, columns)
    mods_recv[me] = mods_send[me]
    for off in range(1, n):
        peer = lax.rem(me + off, n)
        send(mods_send.at[peer], mods_recv.at[me], mods_sems.at[0], mods_sems.at[1], {"tm": peer}).start()

    begin(1)
    tokens = noise_ref.shape[1]
    per = tokens // samples

    current_t, following_t = plan_ref[first + me], plan_ref[first + me + 1]
    shape = (1, tokens)
    bar_current = jnp.full(shape, alpha_ref[current_t], jnp.float32)
    bar_following = jnp.full(shape, alpha_ref[following_t], jnp.float32)
    scale_state = jnp.sqrt(bar_following / bar_current)
    scale_noise = jnp.sqrt(1.0 - bar_following) - scale_state * jnp.sqrt(1.0 - bar_current)

    def spread_terms():
        for way in (0, 1):
            some = mods_recv.at[pl.ds(0, n - 1)]
            copy = send(some, some, mods_sems.at[0], mods_sems.at[1], mate)
            copy.wait_send() if way == 0 else copy.wait_recv()
        flat = mods_recv[...].reshape(n * PAD, columns)
        turned = jnp.transpose(flat).astype(jnp.bfloat16)
        block = columns * 3 // 4
        last = columns - block
        row = lax.broadcasted_iota(jnp.int32, (n * PAD, tokens), 0)
        wanted = lax.broadcasted_iota(jnp.int32, (n * PAD, tokens), 1) // per
        for d in range(n):
            pick = (row == d * PAD + wanted).astype(jnp.bfloat16)
            both = matmul(turned, pick)
            terms[pl.ds(d * block, block)] = both[:block]
            terms[pl.ds(n * block + d * last, last)] = both[block:]

    def term(k):
        return terms[pl.ds(k * width, width)]

    def normal(shift, scale):
        h = hidden[...]
        average = jnp.mean(h, axis=0, keepdims=True)
        centered = h - average
        variance = jnp.mean(centered * centered, axis=0, keepdims=True)
        return (centered / jnp.sqrt(variance + 1e-06) * (1.0 + term(scale)) + term(shift)).astype(jnp.bfloat16)

    def tiles(count, action):
        def step(i, _):
            action(pl.ds(pl.multiple_of(i * ROW_TILE, ROW_TILE), ROW_TILE), i)
            return 0

        lax.fori_loop(0, count // ROW_TILE, step, 0)

    def embed(states):
        pos2 = jnp.concatenate([pos_ref[...]] * (tokens // pos_ref.shape[1]), axis=1)
        hidden[...] = matmul(patch_ref[...], states.astype(jnp.bfloat16)) + pos2

    def project():
        normed = normal(0, 1)

        def action(rows, i):
            projected[rows] = matmul(q_full[rows], normed).astype(jnp.bfloat16)

        tiles(3 * width, action)

    head_dim = width // HEADS
    lanes = 128
    same = (
        lax.broadcasted_iota(jnp.int32, (lanes, lanes), 0) // per
        == lax.broadcasted_iota(jnp.int32, (lanes, lanes), 1) // per
    )

    def attend():
        def one(i, _):
            base = pl.multiple_of(i * head_dim, head_dim)
            for p in range(tokens // lanes):
                cols = pl.ds(p * lanes, lanes)
                q = projected[pl.ds(base, head_dim), cols]
                k = projected[pl.ds(base + width, head_dim), cols]
                v = projected[pl.ds(base + 2 * width, head_dim), cols]
                scores = lax.dot_general(k, q, (((0,), (0,)), ((), ())), preferred_element_type=jnp.float32) / math.sqrt(head_dim)
                raised = jnp.exp(jnp.where(same, scores, -jnp.inf))
                weights = (raised / jnp.sum(raised, axis=0, keepdims=True)).astype(jnp.bfloat16)
                attended[pl.ds(base, head_dim), cols] = matmul(v, weights).astype(jnp.bfloat16)
            return 0

        lax.fori_loop(0, HEADS, one, 0, unroll=2)

    def mix():
        a = attended[...]

        def action(rows, i):
            gate = terms[pl.ds(pl.multiple_of(2 * width + i * ROW_TILE, ROW_TILE), ROW_TILE)]
            hidden[rows] += gate * matmul(m_full[rows], a)

        tiles(width, action)

    def expand():
        normed = normal(3, 4)

        def action(rows, i):
            expanded[rows] = jax.nn.gelu(matmul(e_full[rows], normed), approximate=True).astype(jnp.bfloat16)

        tiles(expanded.shape[0], action)

    def shrink():
        def action(rows, i):
            gate = terms[pl.ds(pl.multiple_of(5 * width + i * ROW_TILE, ROW_TILE), ROW_TILE)]
            hidden[rows] += gate * matmul(s_full[rows], expanded[...])

        tiles(width, action)

    def drift_of(states):
        predicted = matmul(outw_ref[...], normal(6, 7))
        return (scale_state - 1.0) * states + scale_noise * predicted

    planes = n // PLANE
    plane, spot = lax.div(me, PLANE), lax.rem(me, PLANE)

    def earlier(sweep, drift):
        mine = drift.astype(jnp.bfloat16)
        drift_send[sweep] = mine
        drift_recv[sweep, spot] = mine
        for off in range(1, PLANE):
            peer = plane * PLANE + lax.rem(spot + off, PLANE)
            send(drift_send.at[sweep], drift_recv.at[sweep, spot], plane_sems.at[sweep, 0], plane_sems.at[sweep, 1], {"tm": peer}).start()
        some = drift_recv.at[sweep, pl.ds(0, PLANE - 1)]
        send(some, some, plane_sems.at[sweep, 0], plane_sems.at[sweep, 1], mate).wait_recv()
        pieces = [drift_recv[sweep, i].astype(jnp.float32) for i in range(PLANE)]
        total_send[sweep] = functools.reduce(lambda a, b: a + b, pieces).astype(jnp.bfloat16)
        for b in range(1, planes):
            @pl.when(plane < b)
            def _():
                send(total_send.at[sweep], total_recv.at[sweep, plane], total_ssem.at[sweep, b], total_rsem.at[sweep, plane], {"tm": b * PLANE + spot}).start()

        before = jnp.zeros_like(drift)
        for i in range(PLANE - 1):
            before = before + jnp.where(i < spot, pieces[i], 0.0)
        out_ref[...] = before
        for b in range(planes - 1):
            @pl.when(b < plane)
            def _():
                slot = total_recv.at[sweep, b]
                send(slot, slot, total_ssem.at[sweep, b], total_rsem.at[sweep, b], mate).wait_recv()
                out_ref[...] += total_recv[sweep, b].astype(jnp.float32)

        send(some, some, plane_sems.at[sweep, 0], plane_sems.at[sweep, 1], mate).wait_send()
        for b in range(1, planes):
            @pl.when(plane < b)
            def _():
                slot = total_send.at[sweep]
                send(slot, slot, total_ssem.at[sweep, b], total_rsem.at[sweep, 0], mate).wait_send()

        return out_ref[...]

    def arrive(m):
        for hop in range(1, half + 1):
            take(m, hop)
            if hop > 1:
                take_across(m, hop - 1)
        take_across(m, half)
        settle(m)

    noise = noise_ref[...]
    states = noise
    embed(states)
    begin(2)
    spread_terms()
    arrive(0)
    begin(3)
    project()
    attend()
    arrive(1)
    mix()
    arrive(2)
    expand()
    arrive(3)
    shrink()
    drift = drift_of(states)
    states = noise + earlier(0, drift)
    for m in range(4):
        drain(m)
    for sweep in range(1, ITERS):
        embed(states)
        project()
        attend()
        mix()
        expand()
        shrink()
        drift = drift_of(states)
        before = earlier(sweep, drift)
        states = noise + before
    out_ref[...] = states + drift


def fused_body(
    n,
    noise,
    labels,
    timesteps,
    window_start,
    time_weight_in,
    time_weight_out,
    class_table,
    patch_weight,
    query_key_value,
    mix_weight,
    expand_weight,
    shrink_weight,
    block_modulation,
    final_modulation,
    output_weight,
):
    samples, latent = noise.shape
    patch, width = patch_weight.shape
    count = latent // patch
    tokens = samples * count
    hidden_units = shrink_weight.shape[1]
    noise_columns = noise.reshape(tokens, patch).T
    classes = jnp.take(class_table, labels, axis=0, mode="clip")
    classes = jnp.concatenate([classes] * (PAD // samples), axis=0)
    modulation = jnp.concatenate([block_modulation[0], final_modulation], axis=1)
    columns = modulation.shape[1]
    shards = [w[0].T for w in (query_key_value, mix_weight, expand_weight, shrink_weight)]
    table = position_columns(count, width)
    positions = np.concatenate([table] * (128 // count), axis=1)
    half = n // 4
    vmem, smem = pl.BlockSpec(memory_space=pltpu.VMEM), pl.BlockSpec(memory_space=pltpu.SMEM)
    dma = pltpu.SemaphoreType.DMA
    bf16, f32 = jnp.bfloat16, jnp.float32
    out = pl.pallas_call(
        functools.partial(kernel, n, samples),
        out_shape=jax.ShapeDtypeStruct((patch, tokens), f32),
        in_specs=[smem] * 3 + [vmem] * 12,
        out_specs=vmem,
        scratch_shapes=[pltpu.VMEM((s.shape[0] * n, s.shape[1]), bf16) for s in shards]
        + [
            pltpu.VMEM((8 * width, tokens), f32),
            pltpu.VMEM((width, tokens), f32),
            pltpu.VMEM((3 * width, tokens), bf16),
            pltpu.VMEM((width, tokens), bf16),
            pltpu.VMEM((hidden_units, tokens), bf16),
            pltpu.VMEM((n, PAD, columns), f32),
            pltpu.VMEM((n, PAD, columns), f32),
            pltpu.VMEM((ITERS, patch, tokens), bf16),
            pltpu.VMEM((ITERS, PLANE, patch, tokens), bf16),
            pltpu.VMEM((ITERS, patch, tokens), bf16),
            pltpu.VMEM((ITERS, n // PLANE, patch, tokens), bf16),
            dma((4, 2, half)),
            dma((4,)),
            dma((4, 2 * half - 1)),
            dma((4,)),
            dma((4,)),
            dma((4,)),
            dma((4,)),
            dma((2,)),
            dma((ITERS, 2)),
            dma((ITERS, n // PLANE)),
            dma((ITERS, n // PLANE)),
        ],
        compiler_params=pltpu.CompilerParams(
            collective_id=0, has_side_effects=True, vmem_limit_bytes=60 * 1024 * 1024
        ),
    )(
        timesteps,
        window_start,
        jnp.asarray(alpha_table()),
        noise_columns,
        classes,
        time_weight_in,
        time_weight_out,
        modulation,
        patch_weight.T,
        output_weight.T,
        jnp.asarray(positions),
        *shards,
    )
    return out.T.reshape(1, samples, latent)


def fits(n, groups, args):
    rows = [args[i].shape[-1] // n for i in (8, 9, 10, 11)]
    columns = (args[12].shape[-1] + args[13].shape[-1]) // n
    samples = args[0].shape[0] // groups
    count = args[0].shape[1] // args[7].shape[0]
    return (
        groups % 2 == 0
        and n % 8 == 0
        and all(r % 48 == 0 for r in rows)
        and columns % 128 == 0
        and PAD % samples == 0
        and 128 % count == 0
        and samples * count % 128 == 0
        and args[12].shape[-1] == 3 * args[13].shape[-1]
        and args[10].shape[-1] % ROW_TILE == 0
        and args[9].shape[-1] % ROW_TILE == 0
    )


def solution(mesh):
    n, groups = mesh.shape["tm"], mesh.shape["group"]

    def run(*args):
        chosen = functools.partial(fused_body, n) if fits(n, groups, args) else gathered_body
        return shard(chosen, mesh)(*args)

    return run


def shard(body, mesh):
    return jax.shard_map(
        body,
        mesh=mesh,
        in_specs=(
            P("group", None),
            P("group"),
            P(),
            P(),
            P(),
            P(),
            P(),
            P(),
            P(None, None, "tm"),
            P(None, None, "tm"),
            P(None, None, "tm"),
            P(None, None, "tm"),
            P(None, None, "tm"),
            P(None, "tm"),
            P(),
        ),
        out_specs=P("tm", "group", None),
        check_vma=False,
    )
```

```python
import functools
import math

import jax
import jax.numpy as jnp
import numpy as np
from jax import lax
from jax.experimental import pallas as pl
from jax.experimental.pallas import tpu as pltpu
from jax.sharding import PartitionSpec as P

HEADS = 12
ITERS = 2
TRAIN_T = 1000


def carried_in(x, axis, combine, identity):
    count, index = (lax.axis_size(axis), lax.axis_index(axis))
    everything = lax.all_gather(x.astype(jnp.bfloat16), axis)
    start = jnp.broadcast_to(jnp.asarray(identity, x.dtype), x.shape)

    def hop(k, before):
        reached = k < index
        new = combine(before, everything[k].astype(x.dtype))
        return jnp.where(reached, new, before)

    return lax.fori_loop(0, count, hop, start)


def layer_norm(values):
    average = jnp.mean(values, axis=-1, keepdims=True)
    centered = values - average
    variance = jnp.mean(centered * centered, axis=-1, keepdims=True)
    return centered / jnp.sqrt(variance + 1e-06)


def position_table(count, width):
    side = math.isqrt(count)
    quarter = width // 4
    omega = 1.0 / 10000.0 ** (jnp.arange(quarter, dtype=jnp.float32) / quarter)
    index = jnp.arange(count, dtype=jnp.int32)
    first = (index // side).astype(jnp.float32)[:, None] * omega[None, :]
    second = (index % side).astype(jnp.float32)[:, None] * omega[None, :]
    return jnp.concatenate(
        [jnp.sin(first), jnp.cos(first), jnp.sin(second), jnp.cos(second)], axis=1
    )


def plan_terms(timesteps, window_start, step_index, train_steps):
    levels = jnp.arange(train_steps, dtype=jnp.float32)
    betas = 0.0001 + (0.02 - 0.0001) * levels / (train_steps - 1)
    alpha_bar = jnp.cumprod(1.0 - betas)
    current = jnp.take(timesteps, window_start[0] + step_index)
    following = jnp.take(timesteps, window_start[0] + step_index + 1)
    bar_current = jnp.take(alpha_bar, current)
    bar_following = jnp.take(alpha_bar, following)
    scale_state = jnp.sqrt(bar_following / bar_current)
    scale_noise = jnp.sqrt(1.0 - bar_following) - scale_state * jnp.sqrt(1.0 - bar_current)
    return (current, scale_state, scale_noise)


def conditioning(current, labels, time_weight_in, time_weight_out, class_table):
    half = time_weight_in.shape[0] // 2
    rates = jnp.exp(-math.log(10000.0) * jnp.arange(half, dtype=jnp.float32) / half)
    angles = current.astype(jnp.float32)[:, None] * rates[None, :]
    features = jnp.concatenate([jnp.cos(angles), jnp.sin(angles)], axis=1).astype(jnp.bfloat16)
    time_hidden = jax.nn.silu(
        jnp.dot(features, time_weight_in, preferred_element_type=jnp.float32)
    ).astype(jnp.bfloat16)
    time_embed = jnp.dot(time_hidden, time_weight_out, preferred_element_type=jnp.float32)
    selector = (
        labels[:, None] == jnp.arange(class_table.shape[0], dtype=jnp.int32)[None, :]
    ).astype(jnp.bfloat16)
    class_embed = jnp.dot(selector, class_table, preferred_element_type=jnp.float32)
    return jax.nn.silu(time_embed[:, None, :] + class_embed[None, :, :]).astype(jnp.bfloat16)


def network(
    states,
    block_terms,
    final_terms,
    patch_weight,
    query_key_value,
    mix_weight,
    expand_weight,
    shrink_weight,
    output_weight,
    heads,
):
    count = states.shape[0]
    patch = patch_weight.shape[0]
    width = patch_weight.shape[1]
    tokens = states.shape[1] // patch
    head_dim = width // heads
    patches = states.reshape(count * tokens, patch).astype(jnp.bfloat16)
    hidden = jnp.dot(patches, patch_weight, preferred_element_type=jnp.float32).reshape(
        count, tokens, width
    )
    hidden = hidden + position_table(tokens, width)[None]
    blocks = block_terms[0].reshape(count, 6, 1, width)
    normed = (layer_norm(hidden) * (1.0 + blocks[:, 1]) + blocks[:, 0]).astype(jnp.bfloat16)
    projected = jnp.dot(
        normed.reshape(count * tokens, width),
        query_key_value[0],
        preferred_element_type=jnp.float32,
    ).astype(jnp.bfloat16)
    projected = projected.reshape(count, tokens, 3, heads, head_dim)
    scores = jnp.einsum(
        "rqhd,rkhd->rhqk",
        projected[:, :, 0],
        projected[:, :, 1],
        preferred_element_type=jnp.float32,
    ) / math.sqrt(head_dim)
    raised = jnp.exp(scores)
    weights = (raised / jnp.sum(raised, axis=-1, keepdims=True)).astype(jnp.bfloat16)
    attended = jnp.einsum(
        "rhqk,rkhd->rqhd", weights, projected[:, :, 2], preferred_element_type=jnp.float32
    ).astype(jnp.bfloat16)
    mixed = jnp.dot(
        attended.reshape(count * tokens, width), mix_weight[0], preferred_element_type=jnp.float32
    )
    hidden = hidden + blocks[:, 2] * mixed.reshape(count, tokens, width)
    normed = (layer_norm(hidden) * (1.0 + blocks[:, 4]) + blocks[:, 3]).astype(jnp.bfloat16)
    expanded = jax.nn.gelu(
        jnp.dot(
            normed.reshape(count * tokens, width),
            expand_weight[0],
            preferred_element_type=jnp.float32,
        ),
        approximate=True,
    ).astype(jnp.bfloat16)
    shrunk = jnp.dot(expanded, shrink_weight[0], preferred_element_type=jnp.float32)
    hidden = hidden + blocks[:, 5] * shrunk.reshape(count, tokens, width)
    final = final_terms.reshape(count, 2, 1, width)
    normed = (layer_norm(hidden) * (1.0 + final[:, 1]) + final[:, 0]).astype(jnp.bfloat16)
    return jnp.dot(
        normed.reshape(count * tokens, width), output_weight, preferred_element_type=jnp.float32
    ).reshape(count, tokens * patch)


def add_terms(earlier, later):
    return earlier + later


def gathered_body(
    noise,
    labels,
    timesteps,
    window_start,
    time_weight_in,
    time_weight_out,
    class_table,
    patch_weight,
    query_key_value,
    mix_weight,
    expand_weight,
    shrink_weight,
    block_modulation,
    final_modulation,
    output_weight,
):
    position = lax.axis_index("tm")
    current, scale_state, scale_noise = plan_terms(timesteps, window_start, position[None], TRAIN_T)
    condition = conditioning(current, labels, time_weight_in, time_weight_out, class_table)[0]
    full_query, full_mix, full_expand, full_shrink = (
        lax.all_gather(query_key_value, "tm", axis=2, tiled=True),
        lax.all_gather(mix_weight, "tm", axis=2, tiled=True),
        lax.all_gather(expand_weight, "tm", axis=2, tiled=True),
        lax.all_gather(shrink_weight, "tm", axis=2, tiled=True),
    )
    everyone = lax.all_gather(condition, "tm", axis=0, tiled=True)
    block_part = jnp.einsum(
        "rd,ldc->lrc", everyone, block_modulation, preferred_element_type=jnp.float32
    )
    final_part = jnp.dot(everyone, final_modulation, preferred_element_type=jnp.float32)[None]
    block_terms, final_both = (
        lax.all_to_all(
            block_part.astype(jnp.bfloat16), "tm", split_axis=1, concat_axis=2, tiled=True
        ).astype(block_part.dtype),
        lax.all_to_all(
            final_part.astype(jnp.bfloat16), "tm", split_axis=1, concat_axis=2, tiled=True
        ).astype(final_part.dtype),
    )
    final_terms = final_both[0]
    states = noise
    running = noise
    for sweep in range(ITERS):
        predicted = network(
            states,
            block_terms,
            final_terms,
            patch_weight,
            full_query,
            full_mix,
            full_expand,
            full_shrink,
            output_weight,
            HEADS,
        )
        drift = (scale_state[0] - 1.0) * states + scale_noise[0] * predicted
        before = carried_in(drift, "tm", add_terms, jnp.zeros_like(drift))
        running = before + drift
        states = noise + before
    return (noise + running)[None]


PLANE = 4
PAD = 8
ROW_TILE = 256


def alpha_table():
    levels = np.arange(TRAIN_T, dtype=np.float64)
    return np.cumprod(1.0 - (0.0001 + (0.02 - 0.0001) * levels / (TRAIN_T - 1))).astype(np.float32)


def position_columns(count, width):
    side = math.isqrt(count)
    quarter = width // 4
    omega = 1.0 / 10000.0 ** (np.arange(quarter, dtype=np.float64) / quarter)
    index = np.arange(count)
    first = (index // side)[:, None] * omega[None, :]
    second = (index % side)[:, None] * omega[None, :]
    table = np.concatenate([np.sin(first), np.cos(first), np.sin(second), np.cos(second)], axis=1)
    return table.T.astype(np.float32)


def matmul(a, b):
    return jnp.dot(a, b, preferred_element_type=jnp.float32)


def matmul_turned(a, b):
    return lax.dot_general(a, b, (((1,), (1,)), ((), ())), preferred_element_type=jnp.float32)


def turned_matmul(a, b):
    return lax.dot_general(a, b, (((0,), (0,)), ((), ())), preferred_element_type=jnp.float32)


def kernel(
    n,
    samples,
    plan_ref,
    start_ref,
    alpha_ref,
    noise_ref,
    class_ref,
    tin_ref,
    tout_ref,
    modw_ref,
    finalw_ref,
    patch_ref,
    outw_ref,
    pos_ref,
    q_ref,
    m_ref,
    e_ref,
    s_ref,
    out_ref,
    q_full,
    m_full,
    e_full,
    s_full,
    terms,
    hidden,
    projected,
    attended,
    expanded,
    mods_send,
    mods_recv,
    drift_send,
    drift_recv,
    total_send,
    total_recv,
    ring_recv,
    ring_send,
    x_recv,
    x_send,
    mate_recv,
    mate_send,
    local_sem,
    mods_sems,
    plane_sems,
    total_rsem,
    total_ssem,
    before_ref,
):
    me, g = lax.axis_index("tm"), lax.axis_index("group")
    chips = n // 2
    half = chips // 2
    chip, core = lax.div(me, 2), lax.rem(me, 2)
    odd = lax.rem(chip, 2)
    pos = (1 - odd) * lax.div(chip, 2) + odd * (chips - 1 - lax.div(chip, 2))

    def device_at(place):
        place = lax.rem(place + chips, chips)
        upper = lax.div(place, half)
        where = (1 - upper) * (2 * place) + upper * (2 * (chips - 1 - place) + 1)
        return where * 2 + core

    right, left = {"tm": device_at(pos + 1)}, {"tm": device_at(pos - 1)}
    mate = {"tm": me + 1 - 2 * core}
    side = lax.rem(g, 2)
    xmate = {"group": g + 1 - 2 * side}
    fulls, shards = (q_full, m_full, e_full, s_full), (q_ref, m_ref, e_ref, s_ref)

    barrier = pltpu.get_barrier_semaphore()
    for off in range(1, n):
        pl.semaphore_signal(barrier, inc=1, device_id={"tm": lax.rem(me + off, n)}, device_id_type=pl.DeviceIdType.MESH)
    pl.semaphore_signal(barrier, inc=1, device_id=xmate, device_id_type=pl.DeviceIdType.MESH)
    pl.semaphore_wait(barrier, n)

    def send(src, dst, ssem, rsem, target):
        return pltpu.make_async_remote_copy(
            src_ref=src, dst_ref=dst, send_sem=ssem, recv_sem=rsem,
            device_id=target, device_id_type=pl.DeviceIdType.MESH,
        )

    def third(m):
        return shards[m].shape[0] // 3

    def part(m, owner, off, count):
        rows = shards[m].shape[0]
        return fulls[m].at[pl.ds(pl.multiple_of(owner * rows + off, 16), count)]

    def own(m, off, count):
        return shards[m].at[pl.ds(pl.multiple_of(off, 16), count)]

    def begin(m):
        t = third(m)
        off = side * t
        for way, target in ((0, right), (1, left)):
            send(own(m, off, 2 * t), part(m, me, off, 2 * t), ring_send.at[m], ring_recv.at[m, way, 0], target).start()
        send(shards[m], part(m, me, 0, 3 * t), mate_send.at[m], mate_recv.at[m], mate).start()
        pltpu.make_async_copy(shards[m], part(m, me, 0, 3 * t), local_sem.at[m]).start()

    def slab(m, way, hop):
        t = third(m)
        if hop < half:
            return side * t, 2 * t
        return side * t + way * t, t

    def onward(m, hop):
        for way, target in ((0, right), (1, left)):
            owner = device_at(pos - hop) if way == 0 else device_at(pos + hop)
            rows = part(m, owner, *slab(m, way, hop + 1))
            send(rows, rows, ring_send.at[m], ring_recv.at[m, way, hop], target).start()

    def take(m, hop, pass_on=True):
        t = third(m)
        for way, target in ((0, right), (1, left)):
            owner = device_at(pos - hop) if way == 0 else device_at(pos + hop)
            off, count = slab(m, way, hop)
            here = part(m, owner, off, count)
            send(here, here, ring_send.at[m], ring_recv.at[m, way, hop - 1], target).wait_recv()
            if hop < half:
                if pass_on:
                    rows = part(m, owner, *slab(m, way, hop + 1))
                    send(rows, rows, ring_send.at[m], ring_recv.at[m, way, hop], target).start()
                across = part(m, owner, side * 2 * t, t)
                send(across, across, x_send.at[m], x_recv.at[m, 2 * (hop - 1) + way], xmate).start()
            send(here, here, mate_send.at[m], mate_recv.at[m], mate).start()
        if hop == half:
            across = part(m, device_at(pos + half), side * 2 * t, t)
            send(across, across, x_send.at[m], x_recv.at[m, 2 * (half - 1)], xmate).start()

    def take_across(m, hop):
        t = third(m)
        for way in ((0, 1) if hop < half else (0,)):
            owner = device_at(pos - hop) if way == 0 else device_at(pos + hop)
            here = part(m, owner, (1 - side) * 2 * t, t)
            send(here, here, x_send.at[m], x_recv.at[m, 2 * (hop - 1) + way], xmate).wait_recv()
            send(here, here, mate_send.at[m], mate_recv.at[m], mate).start()

    def settle(m):
        rows = shards[m].shape[0]
        everything = fulls[m].at[pl.ds(0, chips * rows)]
        send(everything, everything, mate_send.at[m], mate_recv.at[m], mate).wait_recv()
        pltpu.make_async_copy(shards[m], part(m, me, 0, rows), local_sem.at[m]).wait()

    def drain(m):
        t = third(m)
        for sem, count in ((ring_send, (4 * half - 2) * t), (x_send, (2 * half - 1) * t), (mate_send, 6 * half * t)):
            whole = fulls[m].at[pl.ds(0, count)]
            send(whole, whole, sem.at[m], mate_recv.at[m], mate).wait_send()

    for m in range(4):
        begin(m)

    width = tin_ref.shape[1]
    freq = tin_ref.shape[0]
    first = start_ref[0]
    step_of = lax.broadcasted_iota(jnp.int32, (n * PAD, freq // 2), 0) // PAD
    current = jnp.zeros((n * PAD, freq // 2), jnp.float32)
    for j in range(n):
        current = jnp.where(step_of == j, plan_ref[first + j].astype(jnp.float32), current)
    lane = lax.broadcasted_iota(jnp.int32, (n * PAD, freq // 2), 1).astype(jnp.float32)
    angles = current * jnp.exp(-math.log(10000.0) * lane / (freq // 2))
    features = jnp.concatenate([jnp.cos(angles), jnp.sin(angles)], axis=1).astype(jnp.bfloat16)
    time_hidden = jax.nn.silu(matmul(features, tin_ref[...])).astype(jnp.bfloat16)
    classes = jnp.concatenate([class_ref[...].astype(jnp.float32)] * (PAD // samples), axis=0)
    summed = matmul(time_hidden, tout_ref[...]) + jnp.concatenate([classes] * n, axis=0)
    condition = jax.nn.silu(summed).astype(jnp.bfloat16)
    block, last = modw_ref.shape[0], finalw_ref.shape[0]
    columns = block + last
    pieces = [matmul_turned(condition, modw_ref[...]), matmul_turned(condition, finalw_ref[...])]
    mods_send[...] = jnp.concatenate(pieces, axis=1).reshape(n, PAD, columns)
    mods_recv[me] = mods_send[me]
    for off in range(1, n):
        peer = lax.rem(me + off, n)
        send(mods_send.at[peer], mods_recv.at[me], mods_sems.at[0], mods_sems.at[1], {"tm": peer}).start()

    tokens = noise_ref.shape[0]
    per = tokens // samples

    current_t, following_t = plan_ref[first + me], plan_ref[first + me + 1]
    shape = (1, tokens)
    bar_current = jnp.full(shape, alpha_ref[current_t], jnp.float32)
    bar_following = jnp.full(shape, alpha_ref[following_t], jnp.float32)
    scale_state = jnp.sqrt(bar_following / bar_current)
    scale_noise = jnp.sqrt(1.0 - bar_following) - scale_state * jnp.sqrt(1.0 - bar_current)

    def spread_terms():
        for way in (0, 1):
            some = mods_recv.at[pl.ds(0, n - 1)]
            copy = send(some, some, mods_sems.at[0], mods_sems.at[1], mate)
            copy.wait_send() if way == 0 else copy.wait_recv()
        flat = mods_recv[...].reshape(n * PAD, columns)
        turned = jnp.transpose(flat).astype(jnp.bfloat16)
        row = lax.broadcasted_iota(jnp.int32, (n * PAD, tokens), 0)
        wanted = lax.broadcasted_iota(jnp.int32, (n * PAD, tokens), 1) // per
        for d in range(n):
            pick = (row == d * PAD + wanted).astype(jnp.bfloat16)
            both = matmul(turned, pick)
            terms[pl.ds(d * block, block)] = both[:block]
            terms[pl.ds(n * block + d * last, last)] = both[block:]

    def term(k):
        return terms[pl.ds(k * width, width)]

    def normal(shift, scale):
        h = hidden[...]
        average = jnp.mean(h, axis=0, keepdims=True)
        centered = h - average
        variance = jnp.mean(centered * centered, axis=0, keepdims=True)
        return (centered / jnp.sqrt(variance + 1e-06) * (1.0 + term(scale)) + term(shift)).astype(jnp.bfloat16)

    def tiles(count, action):
        def step(i, _):
            action(pl.ds(pl.multiple_of(i * ROW_TILE, ROW_TILE), ROW_TILE), i)
            return 0

        lax.fori_loop(0, count // ROW_TILE, step, 0)

    def embed(states):
        pos2 = jnp.concatenate([pos_ref[...]] * (tokens // pos_ref.shape[1]), axis=1)
        hidden[...] = turned_matmul(patch_ref[...], states.astype(jnp.bfloat16)) + pos2

    def project():
        normed = normal(0, 1)

        def action(rows, i):
            projected[rows] = matmul(q_full[rows], normed).astype(jnp.bfloat16)

        tiles(3 * width, action)

    head_dim = width // HEADS
    lanes = 128
    same = (
        lax.broadcasted_iota(jnp.int32, (lanes, lanes), 0) // per
        == lax.broadcasted_iota(jnp.int32, (lanes, lanes), 1) // per
    )

    def attend():
        def one(i, _):
            base = pl.multiple_of(i * head_dim, head_dim)
            for p in range(tokens // lanes):
                cols = pl.ds(p * lanes, lanes)
                q = projected[pl.ds(base, head_dim), cols]
                k = projected[pl.ds(base + width, head_dim), cols]
                v = projected[pl.ds(base + 2 * width, head_dim), cols]
                scores = lax.dot_general(k, q, (((0,), (0,)), ((), ())), preferred_element_type=jnp.float32) / math.sqrt(head_dim)
                raised = jnp.exp(jnp.where(same, scores, -jnp.inf))
                weights = (raised / jnp.sum(raised, axis=0, keepdims=True)).astype(jnp.bfloat16)
                attended[pl.ds(base, head_dim), cols] = matmul(v, weights).astype(jnp.bfloat16)
            return 0

        lax.fori_loop(0, HEADS, one, 0, unroll=2)

    def mix():
        a = attended[...]

        def action(rows, i):
            gate = terms[pl.ds(pl.multiple_of(2 * width + i * ROW_TILE, ROW_TILE), ROW_TILE)]
            hidden[rows] += gate * matmul(m_full[rows], a)

        tiles(width, action)

    def expand():
        normed = normal(3, 4)

        def action(rows, i):
            expanded[rows] = jax.nn.gelu(matmul(e_full[rows], normed), approximate=True).astype(jnp.bfloat16)

        tiles(expanded.shape[0], action)

    def shrink():
        def action(rows, i):
            gate = terms[pl.ds(pl.multiple_of(5 * width + i * ROW_TILE, ROW_TILE), ROW_TILE)]
            hidden[rows] += gate * matmul(s_full[rows], expanded[...])

        tiles(width, action)

    def drift_of(states):
        predicted = matmul(outw_ref[...], normal(6, 7))
        return (scale_state - 1.0) * states + scale_noise * predicted

    planes = n // PLANE
    plane, spot = lax.div(me, PLANE), lax.rem(me, PLANE)

    def earlier(sweep, drift):
        mine = drift.astype(jnp.bfloat16)
        drift_send[sweep] = mine
        drift_recv[sweep, spot] = mine
        for off in range(1, PLANE):
            peer = plane * PLANE + lax.rem(spot + off, PLANE)
            send(drift_send.at[sweep], drift_recv.at[sweep, spot], plane_sems.at[sweep, 0], plane_sems.at[sweep, 1], {"tm": peer}).start()
        some = drift_recv.at[sweep, pl.ds(0, PLANE - 1)]
        send(some, some, plane_sems.at[sweep, 0], plane_sems.at[sweep, 1], mate).wait_recv()
        pieces = [drift_recv[sweep, i].astype(jnp.float32) for i in range(PLANE)]
        total_send[sweep] = functools.reduce(lambda a, b: a + b, pieces).astype(jnp.bfloat16)
        for b in range(1, planes):
            @pl.when(plane < b)
            def _():
                send(total_send.at[sweep], total_recv.at[sweep, plane], total_ssem.at[sweep, b], total_rsem.at[sweep, plane], {"tm": b * PLANE + spot}).start()

        before = jnp.zeros_like(drift)
        for i in range(PLANE - 1):
            before = before + jnp.where(i < spot, pieces[i], 0.0)
        before_ref[...] = before
        for b in range(planes - 1):
            @pl.when(b < plane)
            def _():
                slot = total_recv.at[sweep, b]
                send(slot, slot, total_ssem.at[sweep, b], total_rsem.at[sweep, b], mate).wait_recv()
                before_ref[...] += total_recv[sweep, b].astype(jnp.float32)

        send(some, some, plane_sems.at[sweep, 0], plane_sems.at[sweep, 1], mate).wait_send()
        for b in range(1, planes):
            @pl.when(plane < b)
            def _():
                slot = total_send.at[sweep]
                send(slot, slot, total_ssem.at[sweep, b], total_rsem.at[sweep, 0], mate).wait_send()

        return before_ref[...]

    noise = jnp.transpose(noise_ref[...])
    states = noise
    for m in range(3):
        take(m, 1)
    embed(states)
    spread_terms()
    take(3, 1, False)
    for m in range(4):
        take_across(m, 1)
    for hop in range(2, half):
        take(0, hop)
        take(1, hop)
        if hop == 2:
            onward(3, 1)
            take(2, 2, False)
        if hop == 3:
            onward(2, 2)
            take(3, 2)
        if hop > 2:
            take_across(0, hop - 1)
            take_across(1, hop - 1)
    take(0, half)
    take(1, half)
    for m in range(2):
        for hop in range(half - 1, half + 1):
            take_across(m, hop)
    settle(0)
    project()
    attend()
    settle(1)
    mix()
    take_across(2, 2)
    take_across(3, 2)
    for hop in range(3, half):
        take(2, hop)
        take(3, hop)
        take_across(2, hop)
    take(2, half)
    for hop in range(3, half):
        take_across(3, hop)
    take_across(2, half)
    settle(2)
    expand()
    take(3, half)
    take_across(3, half)
    settle(3)
    shrink()
    drift = drift_of(states)
    states = noise + earlier(0, drift)
    for m in range(4):
        drain(m)
    for sweep in range(1, ITERS):
        embed(states)
        project()
        attend()
        mix()
        expand()
        shrink()
        drift = drift_of(states)
        before = earlier(sweep, drift)
        states = noise + before
    out_ref[...] = jnp.transpose(states + drift)


def fused_body(
    n,
    noise,
    labels,
    timesteps,
    window_start,
    time_weight_in,
    time_weight_out,
    class_table,
    patch_weight,
    query_key_value,
    mix_weight,
    expand_weight,
    shrink_weight,
    block_modulation,
    final_modulation,
    output_weight,
):
    samples, latent = noise.shape
    patch, width = patch_weight.shape
    count = latent // patch
    tokens = samples * count
    hidden_units = shrink_weight.shape[1]
    noise_rows = noise.reshape(tokens, patch)
    columns = block_modulation.shape[2] + final_modulation.shape[1]
    shards = [w[0].T for w in (query_key_value, mix_weight, expand_weight, shrink_weight)]
    table = position_columns(count, width)
    positions = np.concatenate([table] * (128 // count), axis=1)
    half = n // 4
    vmem, smem = pl.BlockSpec(memory_space=pltpu.VMEM), pl.BlockSpec(memory_space=pltpu.SMEM)
    dma = pltpu.SemaphoreType.DMA
    bf16, f32 = jnp.bfloat16, jnp.float32
    out = pl.pallas_call(
        functools.partial(kernel, n, samples),
        out_shape=jax.ShapeDtypeStruct((tokens, patch), f32),
        in_specs=[smem] * 3 + [vmem] * 13,
        out_specs=vmem,
        scratch_shapes=[pltpu.VMEM((s.shape[0] * n, s.shape[1]), bf16) for s in shards]
        + [
            pltpu.VMEM((8 * width, tokens), f32),
            pltpu.VMEM((width, tokens), f32),
            pltpu.VMEM((3 * width, tokens), bf16),
            pltpu.VMEM((width, tokens), bf16),
            pltpu.VMEM((hidden_units, tokens), bf16),
            pltpu.VMEM((n, PAD, columns), f32),
            pltpu.VMEM((n, PAD, columns), f32),
            pltpu.VMEM((ITERS, patch, tokens), bf16),
            pltpu.VMEM((ITERS, PLANE, patch, tokens), bf16),
            pltpu.VMEM((ITERS, patch, tokens), bf16),
            pltpu.VMEM((ITERS, n // PLANE, patch, tokens), bf16),
            dma((4, 2, half)),
            dma((4,)),
            dma((4, 2 * half - 1)),
            dma((4,)),
            dma((4,)),
            dma((4,)),
            dma((4,)),
            dma((2,)),
            dma((ITERS, 2)),
            dma((ITERS, n // PLANE)),
            dma((ITERS, n // PLANE)),
            pltpu.VMEM((patch, tokens), f32),
        ],
        compiler_params=pltpu.CompilerParams(
            collective_id=0, has_side_effects=True, vmem_limit_bytes=60 * 1024 * 1024
        ),
    )(
        timesteps,
        window_start,
        jnp.asarray(alpha_table()),
        noise_rows,
        jnp.take(class_table, labels, axis=0, mode="clip"),
        time_weight_in,
        time_weight_out,
        block_modulation[0].T,
        final_modulation.T,
        patch_weight,
        output_weight.T,
        jnp.asarray(positions),
        *shards,
    )
    return out.reshape(1, samples, latent)


def fits(n, groups, args):
    rows = [args[i].shape[-1] // n for i in (8, 9, 10, 11)]
    columns = (args[12].shape[-1] + args[13].shape[-1]) // n
    samples = args[0].shape[0] // groups
    count = args[0].shape[1] // args[7].shape[0]
    return (
        groups % 2 == 0
        and n % 8 == 0
        and n >= 16
        and all(r % 48 == 0 for r in rows)
        and columns % 128 == 0
        and PAD % samples == 0
        and 128 % count == 0
        and samples * count % 128 == 0
        and args[12].shape[-1] == 3 * args[13].shape[-1]
        and args[10].shape[-1] % ROW_TILE == 0
        and args[9].shape[-1] % ROW_TILE == 0
    )


def solution(mesh):
    n, groups = mesh.shape["tm"], mesh.shape["group"]

    def run(*args):
        chosen = functools.partial(fused_body, n) if fits(n, groups, args) else gathered_body
        return shard(chosen, mesh)(*args)

    return run


def shard(body, mesh):
    return jax.shard_map(
        body,
        mesh=mesh,
        in_specs=(
            P("group", None),
            P("group"),
            P(),
            P(),
            P(),
            P(),
            P(),
            P(),
            P(None, None, "tm"),
            P(None, None, "tm"),
            P(None, None, "tm"),
            P(None, None, "tm"),
            P(None, None, "tm"),
            P(None, "tm"),
            P(),
        ),
        out_specs=P("tm", "group", None),
        check_vma=False,
    )
```

```python
import functools
import math

import jax
import jax.numpy as jnp
import numpy as np
from jax import lax
from jax.experimental import pallas as pl
from jax.experimental.pallas import tpu as pltpu
from jax.sharding import PartitionSpec as P

HEADS = 12
ITERS = 2
TRAIN_T = 1000


def carried_in(x, axis, combine, identity):
    count, index = (lax.axis_size(axis), lax.axis_index(axis))
    everything = lax.all_gather(x.astype(jnp.bfloat16), axis)
    start = jnp.broadcast_to(jnp.asarray(identity, x.dtype), x.shape)

    def hop(k, before):
        reached = k < index
        new = combine(before, everything[k].astype(x.dtype))
        return jnp.where(reached, new, before)

    return lax.fori_loop(0, count, hop, start)


def layer_norm(values):
    average = jnp.mean(values, axis=-1, keepdims=True)
    centered = values - average
    variance = jnp.mean(centered * centered, axis=-1, keepdims=True)
    return centered / jnp.sqrt(variance + 1e-06)


def position_table(count, width):
    side = math.isqrt(count)
    quarter = width // 4
    omega = 1.0 / 10000.0 ** (jnp.arange(quarter, dtype=jnp.float32) / quarter)
    index = jnp.arange(count, dtype=jnp.int32)
    first = (index // side).astype(jnp.float32)[:, None] * omega[None, :]
    second = (index % side).astype(jnp.float32)[:, None] * omega[None, :]
    return jnp.concatenate(
        [jnp.sin(first), jnp.cos(first), jnp.sin(second), jnp.cos(second)], axis=1
    )


def plan_terms(timesteps, window_start, step_index, train_steps):
    levels = jnp.arange(train_steps, dtype=jnp.float32)
    betas = 0.0001 + (0.02 - 0.0001) * levels / (train_steps - 1)
    alpha_bar = jnp.cumprod(1.0 - betas)
    current = jnp.take(timesteps, window_start[0] + step_index)
    following = jnp.take(timesteps, window_start[0] + step_index + 1)
    bar_current = jnp.take(alpha_bar, current)
    bar_following = jnp.take(alpha_bar, following)
    scale_state = jnp.sqrt(bar_following / bar_current)
    scale_noise = jnp.sqrt(1.0 - bar_following) - scale_state * jnp.sqrt(1.0 - bar_current)
    return (current, scale_state, scale_noise)


def conditioning(current, labels, time_weight_in, time_weight_out, class_table):
    half = time_weight_in.shape[0] // 2
    rates = jnp.exp(-math.log(10000.0) * jnp.arange(half, dtype=jnp.float32) / half)
    angles = current.astype(jnp.float32)[:, None] * rates[None, :]
    features = jnp.concatenate([jnp.cos(angles), jnp.sin(angles)], axis=1).astype(jnp.bfloat16)
    time_hidden = jax.nn.silu(
        jnp.dot(features, time_weight_in, preferred_element_type=jnp.float32)
    ).astype(jnp.bfloat16)
    time_embed = jnp.dot(time_hidden, time_weight_out, preferred_element_type=jnp.float32)
    selector = (
        labels[:, None] == jnp.arange(class_table.shape[0], dtype=jnp.int32)[None, :]
    ).astype(jnp.bfloat16)
    class_embed = jnp.dot(selector, class_table, preferred_element_type=jnp.float32)
    return jax.nn.silu(time_embed[:, None, :] + class_embed[None, :, :]).astype(jnp.bfloat16)


def network(
    states,
    block_terms,
    final_terms,
    patch_weight,
    query_key_value,
    mix_weight,
    expand_weight,
    shrink_weight,
    output_weight,
    heads,
):
    count = states.shape[0]
    patch = patch_weight.shape[0]
    width = patch_weight.shape[1]
    tokens = states.shape[1] // patch
    head_dim = width // heads
    patches = states.reshape(count * tokens, patch).astype(jnp.bfloat16)
    hidden = jnp.dot(patches, patch_weight, preferred_element_type=jnp.float32).reshape(
        count, tokens, width
    )
    hidden = hidden + position_table(tokens, width)[None]
    blocks = block_terms[0].reshape(count, 6, 1, width)
    normed = (layer_norm(hidden) * (1.0 + blocks[:, 1]) + blocks[:, 0]).astype(jnp.bfloat16)
    projected = jnp.dot(
        normed.reshape(count * tokens, width),
        query_key_value[0],
        preferred_element_type=jnp.float32,
    ).astype(jnp.bfloat16)
    projected = projected.reshape(count, tokens, 3, heads, head_dim)
    scores = jnp.einsum(
        "rqhd,rkhd->rhqk",
        projected[:, :, 0],
        projected[:, :, 1],
        preferred_element_type=jnp.float32,
    ) / math.sqrt(head_dim)
    raised = jnp.exp(scores)
    weights = (raised / jnp.sum(raised, axis=-1, keepdims=True)).astype(jnp.bfloat16)
    attended = jnp.einsum(
        "rhqk,rkhd->rqhd", weights, projected[:, :, 2], preferred_element_type=jnp.float32
    ).astype(jnp.bfloat16)
    mixed = jnp.dot(
        attended.reshape(count * tokens, width), mix_weight[0], preferred_element_type=jnp.float32
    )
    hidden = hidden + blocks[:, 2] * mixed.reshape(count, tokens, width)
    normed = (layer_norm(hidden) * (1.0 + blocks[:, 4]) + blocks[:, 3]).astype(jnp.bfloat16)
    expanded = jax.nn.gelu(
        jnp.dot(
            normed.reshape(count * tokens, width),
            expand_weight[0],
            preferred_element_type=jnp.float32,
        ),
        approximate=True,
    ).astype(jnp.bfloat16)
    shrunk = jnp.dot(expanded, shrink_weight[0], preferred_element_type=jnp.float32)
    hidden = hidden + blocks[:, 5] * shrunk.reshape(count, tokens, width)
    final = final_terms.reshape(count, 2, 1, width)
    normed = (layer_norm(hidden) * (1.0 + final[:, 1]) + final[:, 0]).astype(jnp.bfloat16)
    return jnp.dot(
        normed.reshape(count * tokens, width), output_weight, preferred_element_type=jnp.float32
    ).reshape(count, tokens * patch)


def add_terms(earlier, later):
    return earlier + later


def gathered_body(
    noise,
    labels,
    timesteps,
    window_start,
    time_weight_in,
    time_weight_out,
    class_table,
    patch_weight,
    query_key_value,
    mix_weight,
    expand_weight,
    shrink_weight,
    block_modulation,
    final_modulation,
    output_weight,
):
    position = lax.axis_index("tm")
    current, scale_state, scale_noise = plan_terms(timesteps, window_start, position[None], TRAIN_T)
    condition = conditioning(current, labels, time_weight_in, time_weight_out, class_table)[0]
    full_query, full_mix, full_expand, full_shrink = (
        lax.all_gather(query_key_value, "tm", axis=2, tiled=True),
        lax.all_gather(mix_weight, "tm", axis=2, tiled=True),
        lax.all_gather(expand_weight, "tm", axis=2, tiled=True),
        lax.all_gather(shrink_weight, "tm", axis=2, tiled=True),
    )
    everyone = lax.all_gather(condition, "tm", axis=0, tiled=True)
    block_part = jnp.einsum(
        "rd,ldc->lrc", everyone, block_modulation, preferred_element_type=jnp.float32
    )
    final_part = jnp.dot(everyone, final_modulation, preferred_element_type=jnp.float32)[None]
    block_terms, final_both = (
        lax.all_to_all(
            block_part.astype(jnp.bfloat16), "tm", split_axis=1, concat_axis=2, tiled=True
        ).astype(block_part.dtype),
        lax.all_to_all(
            final_part.astype(jnp.bfloat16), "tm", split_axis=1, concat_axis=2, tiled=True
        ).astype(final_part.dtype),
    )
    final_terms = final_both[0]
    states = noise
    running = noise
    for sweep in range(ITERS):
        predicted = network(
            states,
            block_terms,
            final_terms,
            patch_weight,
            full_query,
            full_mix,
            full_expand,
            full_shrink,
            output_weight,
            HEADS,
        )
        drift = (scale_state[0] - 1.0) * states + scale_noise[0] * predicted
        before = carried_in(drift, "tm", add_terms, jnp.zeros_like(drift))
        running = before + drift
        states = noise + before
    return (noise + running)[None]


PLANE = 4
PAD = 8
ROW_TILE = 256


def alpha_table():
    levels = np.arange(TRAIN_T, dtype=np.float64)
    return np.cumprod(1.0 - (0.0001 + (0.02 - 0.0001) * levels / (TRAIN_T - 1))).astype(np.float32)


def position_columns(count, width):
    side = math.isqrt(count)
    quarter = width // 4
    omega = 1.0 / 10000.0 ** (np.arange(quarter, dtype=np.float64) / quarter)
    index = np.arange(count)
    first = (index // side)[:, None] * omega[None, :]
    second = (index % side)[:, None] * omega[None, :]
    table = np.concatenate([np.sin(first), np.cos(first), np.sin(second), np.cos(second)], axis=1)
    return table.T.astype(np.float32)


def matmul(a, b):
    return jnp.dot(a, b, preferred_element_type=jnp.float32)


def matmul_turned(a, b):
    return lax.dot_general(a, b, (((1,), (1,)), ((), ())), preferred_element_type=jnp.float32)


def turned_matmul(a, b):
    return lax.dot_general(a, b, (((0,), (0,)), ((), ())), preferred_element_type=jnp.float32)


def kernel(
    n,
    samples,
    plan_ref,
    start_ref,
    alpha_ref,
    noise_ref,
    class_ref,
    tin_ref,
    tout_ref,
    modw_ref,
    finalw_ref,
    patch_ref,
    outw_ref,
    pos_ref,
    q_ref,
    m_ref,
    e_ref,
    s_ref,
    out_ref,
    q_full,
    m_full,
    e_full,
    s_full,
    terms,
    hidden,
    projected,
    attended,
    expanded,
    mods_send,
    mods_recv,
    drift_send,
    drift_recv,
    total_send,
    total_recv,
    ring_recv,
    ring_send,
    x_recv,
    x_send,
    mate_recv,
    mate_send,
    local_sem,
    mods_sems,
    plane_sems,
    total_rsem,
    total_ssem,
    before_ref,
):
    me, g = lax.axis_index("tm"), lax.axis_index("group")
    chips = n // 2
    half = chips // 2
    chip, core = lax.div(me, 2), lax.rem(me, 2)
    odd = lax.rem(chip, 2)
    pos = (1 - odd) * lax.div(chip, 2) + odd * (chips - 1 - lax.div(chip, 2))

    def device_at(place):
        place = lax.rem(place + chips, chips)
        upper = lax.div(place, half)
        where = (1 - upper) * (2 * place) + upper * (2 * (chips - 1 - place) + 1)
        return where * 2 + core

    right, left = {"tm": device_at(pos + 1)}, {"tm": device_at(pos - 1)}
    mate = {"tm": me + 1 - 2 * core}
    side = lax.rem(g, 2)
    xmate = {"group": g + 1 - 2 * side}
    fulls, shards = (q_full, m_full, e_full, s_full), (q_ref, m_ref, e_ref, s_ref)

    barrier = pltpu.get_barrier_semaphore()
    for off in range(1, n):
        pl.semaphore_signal(barrier, inc=1, device_id={"tm": lax.rem(me + off, n)}, device_id_type=pl.DeviceIdType.MESH)
    pl.semaphore_signal(barrier, inc=1, device_id=xmate, device_id_type=pl.DeviceIdType.MESH)
    pl.semaphore_wait(barrier, n)

    def send(src, dst, ssem, rsem, target):
        return pltpu.make_async_remote_copy(
            src_ref=src, dst_ref=dst, send_sem=ssem, recv_sem=rsem,
            device_id=target, device_id_type=pl.DeviceIdType.MESH,
        )

    def third(m):
        return shards[m].shape[0] // 3

    def part(m, owner, off, count):
        rows = shards[m].shape[0]
        return fulls[m].at[pl.ds(pl.multiple_of(owner * rows + off, 16), count)]

    def own(m, off, count):
        return shards[m].at[pl.ds(pl.multiple_of(off, 16), count)]

    def begin(m):
        t = third(m)
        off = side * t
        for way, target in ((0, right), (1, left)):
            send(own(m, off, 2 * t), part(m, me, off, 2 * t), ring_send.at[m], ring_recv.at[m, way, 0], target).start()
        send(shards[m], part(m, me, 0, 3 * t), mate_send.at[m], mate_recv.at[m], mate).start()
        pltpu.make_async_copy(shards[m], part(m, me, 0, 3 * t), local_sem.at[m]).start()

    def slab(m, way, hop):
        t = third(m)
        if hop < half:
            return side * t, 2 * t
        return side * t + way * t, t

    def onward(m, hop):
        for way, target in ((0, right), (1, left)):
            owner = device_at(pos - hop) if way == 0 else device_at(pos + hop)
            rows = part(m, owner, *slab(m, way, hop + 1))
            send(rows, rows, ring_send.at[m], ring_recv.at[m, way, hop], target).start()

    def take(m, hop, pass_on=True):
        t = third(m)
        for way, target in ((0, right), (1, left)):
            owner = device_at(pos - hop) if way == 0 else device_at(pos + hop)
            off, count = slab(m, way, hop)
            here = part(m, owner, off, count)
            send(here, here, ring_send.at[m], ring_recv.at[m, way, hop - 1], target).wait_recv()
            if hop < half:
                if pass_on:
                    rows = part(m, owner, *slab(m, way, hop + 1))
                    send(rows, rows, ring_send.at[m], ring_recv.at[m, way, hop], target).start()
                across = part(m, owner, side * 2 * t, t)
                send(across, across, x_send.at[m], x_recv.at[m, 2 * (hop - 1) + way], xmate).start()
            send(here, here, mate_send.at[m], mate_recv.at[m], mate).start()
        if hop == half:
            across = part(m, device_at(pos + half), side * 2 * t, t)
            send(across, across, x_send.at[m], x_recv.at[m, 2 * (half - 1)], xmate).start()

    def take_across(m, hop):
        t = third(m)
        for way in ((0, 1) if hop < half else (0,)):
            owner = device_at(pos - hop) if way == 0 else device_at(pos + hop)
            here = part(m, owner, (1 - side) * 2 * t, t)
            send(here, here, x_send.at[m], x_recv.at[m, 2 * (hop - 1) + way], xmate).wait_recv()
            send(here, here, mate_send.at[m], mate_recv.at[m], mate).start()

    def settle(m):
        rows = shards[m].shape[0]
        everything = fulls[m].at[pl.ds(0, chips * rows)]
        send(everything, everything, mate_send.at[m], mate_recv.at[m], mate).wait_recv()
        pltpu.make_async_copy(shards[m], part(m, me, 0, rows), local_sem.at[m]).wait()

    def drain(m):
        t = third(m)
        for sem, count in ((ring_send, (4 * half - 2) * t), (x_send, (2 * half - 1) * t), (mate_send, 6 * half * t)):
            whole = fulls[m].at[pl.ds(0, count)]
            send(whole, whole, sem.at[m], mate_recv.at[m], mate).wait_send()

    for m in range(4):
        begin(m)
    take(0, 1)
    take(1, 1)

    width = tin_ref.shape[1]
    freq = tin_ref.shape[0]
    first = start_ref[0]
    step_of = lax.broadcasted_iota(jnp.int32, (n * PAD, freq // 2), 0) // PAD
    current = jnp.zeros((n * PAD, freq // 2), jnp.float32)
    for j in range(n):
        current = jnp.where(step_of == j, plan_ref[first + j].astype(jnp.float32), current)
    lane = lax.broadcasted_iota(jnp.int32, (n * PAD, freq // 2), 1).astype(jnp.float32)
    angles = current * jnp.exp(-math.log(10000.0) * lane / (freq // 2))
    features = jnp.concatenate([jnp.cos(angles), jnp.sin(angles)], axis=1).astype(jnp.bfloat16)
    time_hidden = jax.nn.silu(matmul(features, tin_ref[...])).astype(jnp.bfloat16)
    classes = jnp.concatenate([class_ref[...].astype(jnp.float32)] * (PAD // samples), axis=0)
    summed = matmul(time_hidden, tout_ref[...]) + jnp.concatenate([classes] * n, axis=0)
    condition = jax.nn.silu(summed).astype(jnp.bfloat16)
    block, last = modw_ref.shape[0], finalw_ref.shape[0]
    columns = block + last
    pieces = [matmul_turned(condition, modw_ref[...]), matmul_turned(condition, finalw_ref[...])]
    mods_send[...] = jnp.concatenate(pieces, axis=1).reshape(n, PAD, columns)
    mods_recv[me] = mods_send[me]
    for off in range(1, n):
        peer = lax.rem(me + off, n)
        send(mods_send.at[peer], mods_recv.at[me], mods_sems.at[0], mods_sems.at[1], {"tm": peer}).start()

    tokens = noise_ref.shape[0]
    per = tokens // samples

    current_t, following_t = plan_ref[first + me], plan_ref[first + me + 1]
    shape = (1, tokens)
    bar_current = jnp.full(shape, alpha_ref[current_t], jnp.float32)
    bar_following = jnp.full(shape, alpha_ref[following_t], jnp.float32)
    scale_state = jnp.sqrt(bar_following / bar_current)
    scale_noise = jnp.sqrt(1.0 - bar_following) - scale_state * jnp.sqrt(1.0 - bar_current)

    def spread_terms():
        for way in (0, 1):
            some = mods_recv.at[pl.ds(0, n - 1)]
            copy = send(some, some, mods_sems.at[0], mods_sems.at[1], mate)
            copy.wait_send() if way == 0 else copy.wait_recv()
        flat = mods_recv[...].reshape(n * PAD, columns)
        turned = jnp.transpose(flat).astype(jnp.bfloat16)
        row = lax.broadcasted_iota(jnp.int32, (n * PAD, tokens), 0)
        wanted = lax.broadcasted_iota(jnp.int32, (n * PAD, tokens), 1) // per
        for d in range(n):
            pick = (row == d * PAD + wanted).astype(jnp.bfloat16)
            both = matmul(turned, pick)
            terms[pl.ds(d * block, block)] = both[:block]
            terms[pl.ds(n * block + d * last, last)] = both[block:]

    def term(k):
        return terms[pl.ds(k * width, width)]

    def normal(shift, scale):
        h = hidden[...]
        average = jnp.mean(h, axis=0, keepdims=True)
        centered = h - average
        variance = jnp.mean(centered * centered, axis=0, keepdims=True)
        return (centered / jnp.sqrt(variance + 1e-06) * (1.0 + term(scale)) + term(shift)).astype(jnp.bfloat16)

    def tiles(count, action):
        def step(i, _):
            action(pl.ds(pl.multiple_of(i * ROW_TILE, ROW_TILE), ROW_TILE), i)
            return 0

        lax.fori_loop(0, count // ROW_TILE, step, 0, unroll=3)

    def embed(states):
        pos2 = jnp.concatenate([pos_ref[...]] * (tokens // pos_ref.shape[1]), axis=1)
        hidden[...] = turned_matmul(patch_ref[...], states.astype(jnp.bfloat16)) + pos2

    def project():
        normed = normal(0, 1)

        def action(rows, i):
            projected[rows] = matmul(q_full[rows], normed).astype(jnp.bfloat16)

        tiles(3 * width, action)

    head_dim = width // HEADS
    lanes = 128
    same = (
        lax.broadcasted_iota(jnp.int32, (lanes, lanes), 0) // per
        == lax.broadcasted_iota(jnp.int32, (lanes, lanes), 1) // per
    )

    def attend():
        def one(i, _):
            base = pl.multiple_of(i * head_dim, head_dim)
            for p in range(tokens // lanes):
                cols = pl.ds(p * lanes, lanes)
                q = projected[pl.ds(base, head_dim), cols]
                k = projected[pl.ds(base + width, head_dim), cols]
                v = projected[pl.ds(base + 2 * width, head_dim), cols]
                scores = lax.dot_general(k, q, (((0,), (0,)), ((), ())), preferred_element_type=jnp.float32) / math.sqrt(head_dim)
                raised = jnp.exp(jnp.where(same, scores, -jnp.inf))
                weights = (raised / jnp.sum(raised, axis=0, keepdims=True)).astype(jnp.bfloat16)
                attended[pl.ds(base, head_dim), cols] = matmul(v, weights).astype(jnp.bfloat16)
            return 0

        lax.fori_loop(0, HEADS, one, 0, unroll=4)

    def mix():
        a = attended[...]

        def action(rows, i):
            gate = terms[pl.ds(pl.multiple_of(2 * width + i * ROW_TILE, ROW_TILE), ROW_TILE)]
            hidden[rows] += gate * matmul(m_full[rows], a)

        tiles(width, action)

    def expand():
        normed = normal(3, 4)

        def action(rows, i):
            expanded[rows] = jax.nn.gelu(matmul(e_full[rows], normed), approximate=True).astype(jnp.bfloat16)

        tiles(expanded.shape[0], action)

    def shrink():
        def action(rows, i):
            gate = terms[pl.ds(pl.multiple_of(5 * width + i * ROW_TILE, ROW_TILE), ROW_TILE)]
            hidden[rows] += gate * matmul(s_full[rows], expanded[...])

        tiles(width, action)

    def drift_of(states):
        predicted = matmul(outw_ref[...], normal(6, 7))
        return (scale_state - 1.0) * states + scale_noise * predicted

    planes = n // PLANE
    plane, spot = lax.div(me, PLANE), lax.rem(me, PLANE)

    def earlier(sweep, drift):
        mine = drift.astype(jnp.bfloat16)
        drift_send[sweep] = mine
        drift_recv[sweep, spot] = mine
        for off in range(1, PLANE):
            peer = plane * PLANE + lax.rem(spot + off, PLANE)
            send(drift_send.at[sweep], drift_recv.at[sweep, spot], plane_sems.at[sweep, 0], plane_sems.at[sweep, 1], {"tm": peer}).start()
        some = drift_recv.at[sweep, pl.ds(0, PLANE - 1)]
        send(some, some, plane_sems.at[sweep, 0], plane_sems.at[sweep, 1], mate).wait_recv()
        pieces = [drift_recv[sweep, i].astype(jnp.float32) for i in range(PLANE)]
        total_send[sweep] = functools.reduce(lambda a, b: a + b, pieces).astype(jnp.bfloat16)
        for b in range(1, planes):
            @pl.when(plane < b)
            def _():
                send(total_send.at[sweep], total_recv.at[sweep, plane], total_ssem.at[sweep, b], total_rsem.at[sweep, plane], {"tm": b * PLANE + spot}).start()

        before = jnp.zeros_like(drift)
        for i in range(PLANE - 1):
            before = before + jnp.where(i < spot, pieces[i], 0.0)
        before_ref[...] = before
        for b in range(planes - 1):
            @pl.when(b < plane)
            def _():
                slot = total_recv.at[sweep, b]
                send(slot, slot, total_ssem.at[sweep, b], total_rsem.at[sweep, b], mate).wait_recv()
                before_ref[...] += total_recv[sweep, b].astype(jnp.float32)

        send(some, some, plane_sems.at[sweep, 0], plane_sems.at[sweep, 1], mate).wait_send()
        for b in range(1, planes):
            @pl.when(plane < b)
            def _():
                slot = total_send.at[sweep]
                send(slot, slot, total_ssem.at[sweep, b], total_rsem.at[sweep, 0], mate).wait_send()

        return before_ref[...]

    noise = jnp.transpose(noise_ref[...])
    states = noise
    take(2, 1)
    embed(states)
    take(3, 1, False)
    spread_terms()
    for m in range(4):
        take_across(m, 1)
    for hop in range(2, half):
        take(0, hop)
        take(1, hop)
        if hop == 2:
            onward(3, 1)
            take(2, 2, False)
        if hop == 3:
            onward(2, 2)
            take(3, 2)
        if hop > 2:
            take_across(0, hop - 1)
            take_across(1, hop - 1)
    take(0, half)
    take(1, half)
    for m in range(2):
        for hop in range(half - 1, half + 1):
            take_across(m, hop)
    settle(0)
    project()
    attend()
    settle(1)
    mix()
    take_across(2, 2)
    take_across(3, 2)
    for hop in range(3, half):
        take(2, hop)
        take(3, hop)
        take_across(2, hop)
    take(2, half)
    for hop in range(3, half):
        take_across(3, hop)
    take_across(2, half)
    settle(2)
    expand()
    take(3, half)
    take_across(3, half)
    settle(3)
    shrink()
    drift = drift_of(states)
    states = noise + earlier(0, drift)
    for m in range(4):
        drain(m)
    for sweep in range(1, ITERS):
        embed(states)
        project()
        attend()
        mix()
        expand()
        shrink()
        drift = drift_of(states)
        before = earlier(sweep, drift)
        states = noise + before
    out_ref[...] = jnp.transpose(states + drift)


def fused_body(
    n,
    noise,
    labels,
    timesteps,
    window_start,
    time_weight_in,
    time_weight_out,
    class_table,
    patch_weight,
    query_key_value,
    mix_weight,
    expand_weight,
    shrink_weight,
    block_modulation,
    final_modulation,
    output_weight,
):
    samples, latent = noise.shape
    patch, width = patch_weight.shape
    count = latent // patch
    tokens = samples * count
    hidden_units = shrink_weight.shape[1]
    noise_rows = noise.reshape(tokens, patch)
    columns = block_modulation.shape[2] + final_modulation.shape[1]
    shards = [w[0].T for w in (query_key_value, mix_weight, expand_weight, shrink_weight)]
    table = position_columns(count, width)
    positions = np.concatenate([table] * (128 // count), axis=1)
    half = n // 4
    vmem, smem = pl.BlockSpec(memory_space=pltpu.VMEM), pl.BlockSpec(memory_space=pltpu.SMEM)
    dma = pltpu.SemaphoreType.DMA
    bf16, f32 = jnp.bfloat16, jnp.float32
    out = pl.pallas_call(
        functools.partial(kernel, n, samples),
        out_shape=jax.ShapeDtypeStruct((tokens, patch), f32),
        in_specs=[smem] * 3 + [vmem] * 13,
        out_specs=vmem,
        scratch_shapes=[pltpu.VMEM((s.shape[0] * n, s.shape[1]), bf16) for s in shards]
        + [
            pltpu.VMEM((8 * width, tokens), f32),
            pltpu.VMEM((width, tokens), f32),
            pltpu.VMEM((3 * width, tokens), bf16),
            pltpu.VMEM((width, tokens), bf16),
            pltpu.VMEM((hidden_units, tokens), bf16),
            pltpu.VMEM((n, PAD, columns), f32),
            pltpu.VMEM((n, PAD, columns), f32),
            pltpu.VMEM((ITERS, patch, tokens), bf16),
            pltpu.VMEM((ITERS, PLANE, patch, tokens), bf16),
            pltpu.VMEM((ITERS, patch, tokens), bf16),
            pltpu.VMEM((ITERS, n // PLANE, patch, tokens), bf16),
            dma((4, 2, half)),
            dma((4,)),
            dma((4, 2 * half - 1)),
            dma((4,)),
            dma((4,)),
            dma((4,)),
            dma((4,)),
            dma((2,)),
            dma((ITERS, 2)),
            dma((ITERS, n // PLANE)),
            dma((ITERS, n // PLANE)),
            pltpu.VMEM((patch, tokens), f32),
        ],
        compiler_params=pltpu.CompilerParams(
            collective_id=0, has_side_effects=True, vmem_limit_bytes=60 * 1024 * 1024
        ),
    )(
        timesteps,
        window_start,
        jnp.asarray(alpha_table()),
        noise_rows,
        jnp.take(class_table, labels, axis=0, mode="clip"),
        time_weight_in,
        time_weight_out,
        block_modulation[0].T,
        final_modulation.T,
        patch_weight,
        output_weight.T,
        jnp.asarray(positions),
        *shards,
    )
    return out.reshape(1, samples, latent)


def fits(n, groups, args):
    rows = [args[i].shape[-1] // n for i in (8, 9, 10, 11)]
    columns = (args[12].shape[-1] + args[13].shape[-1]) // n
    samples = args[0].shape[0] // groups
    count = args[0].shape[1] // args[7].shape[0]
    return (
        groups % 2 == 0
        and n % 8 == 0
        and n >= 16
        and all(r % 48 == 0 for r in rows)
        and columns % 128 == 0
        and PAD % samples == 0
        and 128 % count == 0
        and samples * count % 128 == 0
        and args[12].shape[-1] == 3 * args[13].shape[-1]
        and args[10].shape[-1] % ROW_TILE == 0
        and args[9].shape[-1] % ROW_TILE == 0
    )


def solution(mesh):
    n, groups = mesh.shape["tm"], mesh.shape["group"]

    def run(*args):
        chosen = functools.partial(fused_body, n) if fits(n, groups, args) else gathered_body
        return shard(chosen, mesh)(*args)

    return run


def shard(body, mesh):
    return jax.shard_map(
        body,
        mesh=mesh,
        in_specs=(
            P("group", None),
            P("group"),
            P(),
            P(),
            P(),
            P(),
            P(),
            P(),
            P(None, None, "tm"),
            P(None, None, "tm"),
            P(None, None, "tm"),
            P(None, None, "tm"),
            P(None, None, "tm"),
            P(None, "tm"),
            P(),
        ),
        out_specs=P("tm", "group", None),
        check_vma=False,
    )
```
